32 devices in a mesh: ri: 8 (over z, core), rj: 4 (over y, x).
Axes of the slice: x: 2, y: 2, z: 4, core: 2. Of those that a mesh axis runs over, the one named last changes fastest.
Arguments:
- pair: bfloat16 [320, 320, 128], P('ri', 'rj'), may hold values from -6 to 6
- in_gain: float32 [128], replicated, may hold values from 0.1 to 1.9
- in_bias: float32 [128], replicated, may hold values from -3 to 3
- w_in: bfloat16 [128, 512], replicated, may hold values from -0.5 to 0.5
- w_gate: bfloat16 [128, 128], replicated, may hold values from -0.5 to 0.5
- out_gain: float32 [128], replicated, may hold values from 0.1 to 1.9
- out_bias: float32 [128], replicated, may hold values from -3 to 3
- w_out: bfloat16 [128, 128], replicated, may hold values from -0.5 to 0.5
Outputs:
- update: bfloat16 [320, 320, 128], P('ri', 'rj')
The draws below stay inside these ranges and needn't reach their ends.
All inputs are finite; a program needn't handle non-finite values.
Results may differ from the reference program's by a relative error of at most 0.015.
Values may be sent and summed in bfloat16 or wider, within the bound.
A program may use at most 128 MiB of HBM per device.

```python
import jax
import jax.numpy as jnp
from jax import lax

C = 128
H = 128
NR = 320


def steps_of(own_key, extent, shards, least, top_value):
    level, own = 1.0, jax.random.fold_in(own_key, 6)
    for dim, parts in shards:
        steps = jnp.exp(jax.random.uniform(jax.random.fold_in(own, dim), (parts,), jnp.float32, least / len(shards), top_value / len(shards)))
        level = level * jnp.repeat(steps, extent[dim] // parts).reshape([-1 if axis == dim else 1 for axis in range(len(extent))])
    return level


def normal_values(stream_key, shape, width, bound, cuts=(), dtype=jnp.bfloat16):
    level = steps_of(stream_key, shape, cuts, -0.22, 0.18) if cuts else 1.0
    drawn = jax.random.normal(stream_key, shape, jnp.float32) * width * level
    return jnp.minimum(jnp.maximum(drawn, -bound), bound).astype(dtype)


def setup_inputs(seed: int = 0) -> dict:
    splits = jax.random.split(jax.random.key(seed), 9)
    pair = normal_values(splits[0], (NR, NR, C), 1.0, 6.0, ((0, 8), (1, 4)))
    in_gain = jnp.clip(1.0 + 0.18 * jax.random.normal(splits[1], (C,), jnp.float32), 0.1, 1.9)
    in_bias = normal_values(splits[2], (C,), 0.5, 3.0, (), jnp.float32)
    w_in = normal_values(splits[3], (C, 4 * H), C ** -0.5, 0.5)
    w_gate = normal_values(splits[4], (C, C), C ** -0.5, 0.5)
    out_gain = jnp.clip(1.0 + 0.18 * jax.random.normal(splits[5], (H,), jnp.float32), 0.1, 1.9)
    out_bias = normal_values(splits[6], (H,), 0.5, 3.0, (), jnp.float32)
    w_out = normal_values(splits[7], (H, C), H ** -0.5, 0.5)
    return dict(pair=pair, in_gain=in_gain, in_bias=in_bias, w_in=w_in, w_gate=w_gate, out_gain=out_gain, out_bias=out_bias, w_out=w_out)


def layer_norm(values, gain, bias):
    mean = lax.optimization_barrier(jnp.mean(values, axis=-1, keepdims=True))
    centered = values - mean
    var = lax.optimization_barrier(jnp.mean(centered * centered, axis=-1, keepdims=True))
    return centered * lax.rsqrt(var + 1e-05) * gain + bias

def reference(pair, in_gain, in_bias, w_in, w_gate, out_gain, out_bias, w_out):
    normed = layer_norm(pair.astype(jnp.float32), in_gain, in_bias).astype(jnp.bfloat16)
    flat = normed.reshape(NR * NR, C)
    proj = jnp.dot(flat, w_in, preferred_element_type=jnp.float32)
    a_vals = (jax.nn.sigmoid(proj[:, H:2 * H]) * proj[:, :H]).astype(jnp.bfloat16).reshape(NR, NR, H)
    b_vals = (jax.nn.sigmoid(proj[:, 3 * H:]) * proj[:, 2 * H:3 * H]).astype(jnp.bfloat16).reshape(NR, NR, H)
    gate = jax.nn.sigmoid(jnp.dot(flat, w_gate, preferred_element_type=jnp.float32)).astype(jnp.bfloat16)
    tri = jnp.einsum('kic,kjc->ijc', a_vals.astype(jnp.float32), b_vals.astype(jnp.float32))
    tri_normed = layer_norm(tri, out_gain, out_bias).astype(jnp.bfloat16).reshape(NR * NR, H)
    mixed = jnp.dot(tri_normed, w_out, preferred_element_type=jnp.float32)
    update = gate.astype(jnp.float32) * mixed
    return update.reshape(NR, NR, C).astype(jnp.bfloat16)
```

```python
import jax
import jax.numpy as jnp
from jax import lax
from jax.sharding import PartitionSpec as P

AXES = ("ri", "rj")


def layer_norm(values, gain, bias, axis):
    mean = jnp.mean(values, axis=axis, keepdims=True)
    centered = values - mean
    var = jnp.mean(centered * centered, axis=axis, keepdims=True)
    return centered * lax.rsqrt(var + 1e-05) * gain + bias


def exchange(blocks):
    return lax.all_to_all(blocks, AXES, 0, 0, tiled=True)


def local(n_ri, n_rj, pair, in_gain, in_bias, w_in, w_gate, out_gain, out_bias, w_out):
    rows, cols, chans = pair.shape
    hidden = w_out.shape[0]
    n = n_ri * n_rj
    own = hidden // n
    spots = rows * cols
    flat = layer_norm(
        pair.reshape(spots, chans).astype(jnp.float32), in_gain, in_bias, -1
    ).astype(jnp.bfloat16)
    proj = lax.dot_general(
        w_in, flat, (((0,), (1,)), ((), ())), preferred_element_type=jnp.float32
    ).reshape(4, n, own, spots)
    a_blocks = (jax.nn.sigmoid(proj[1]) * proj[0]).astype(jnp.bfloat16)
    b_blocks = (jax.nn.sigmoid(proj[3]) * proj[2]).astype(jnp.bfloat16)
    got = exchange(jnp.concatenate([a_blocks, b_blocks], axis=1))
    gate = jax.nn.sigmoid(jnp.dot(flat, w_gate, preferred_element_type=jnp.float32)).astype(
        jnp.bfloat16
    )
    got = got.reshape(n_ri, n_rj, 2, own, rows, cols)
    got = jnp.transpose(got, (2, 3, 0, 4, 1, 5)).reshape(2, own, n_ri * rows, n_rj * cols)
    product = lax.dot_general(
        got[0], got[1], (((1,), (1,)), ((0,), (0,))), preferred_element_type=jnp.float32
    ).astype(jnp.bfloat16)
    product = product.reshape(own, n_ri, rows, n_rj, cols)
    product = jnp.transpose(product, (1, 3, 0, 2, 4)).reshape(n, own, spots)
    tri = exchange(product).reshape(hidden, spots).astype(jnp.float32)
    tri_normed = layer_norm(tri, out_gain[:, None], out_bias[:, None], 0).astype(jnp.bfloat16)
    mixed = lax.dot_general(
        tri_normed, w_out, (((0,), (0,)), ((), ())), preferred_element_type=jnp.float32
    )
    update = gate.astype(jnp.float32) * mixed
    return update.reshape(rows, cols, chans).astype(jnp.bfloat16)


def solution(mesh):
    n_ri, n_rj = mesh.shape["ri"], mesh.shape["rj"]
    return jax.shard_map(
        lambda *args: local(n_ri, n_rj, *args),
        mesh=mesh,
        in_specs=(P("ri", "rj", None), P(), P(), P(), P(), P(), P(), P()),
        out_specs=P("ri", "rj", None),
        check_vma=False,
    )
```

```python
import functools

import jax
import jax.numpy as jnp
from jax import lax
from jax.experimental import pallas as pl
from jax.experimental.pallas import tpu as pltpu
from jax.sharding import PartitionSpec as P

MESH = pl.DeviceIdType.MESH
LANES = 128


def shifted(vregs, start):
    at, by = divmod(start, LANES)
    if by == 0:
        return vregs[at]
    return pltpu.roll(vregs[at], LANES - by, 1)


def body(n_ri, n_rj, rows, cols, own, pair, gain, bias, w_in, w_gate, gate_ref, out_ref,
         flat_s, ab_s, x_s, recv_s, g_s, b_s, o_s, t_s,
         send1, recv1, send2, recv2, loc):
    n = n_ri * n_rj
    spots = rows * cols
    depth = n_ri * rows
    hidden = n * own
    halves = cols // rows
    ri, rj = lax.axis_index("ri"), lax.axis_index("rj")
    me = ri * n_rj + rj

    def other(d):
        return lax.rem(me + d, n)

    barrier = pltpu.get_barrier_semaphore()

    def greet(d, _):
        to = other(d)
        pl.semaphore_signal(
            barrier, inc=1, device_id=(to // n_rj, lax.rem(to, n_rj)), device_id_type=MESH
        )
        return _

    lax.fori_loop(1, n, greet, 0)

    wt = w_in[...].T
    step = spots // 5

    def project(i, _):
        at = pl.multiple_of(i * step, LANES)
        x = pair[pl.ds(at, step), :].astype(jnp.float32)
        mean = jnp.mean(x, axis=-1, keepdims=True)
        centered = x - mean
        var = jnp.mean(centered * centered, axis=-1, keepdims=True)
        flat = (centered * lax.rsqrt(var + 1e-05) * gain[...] + bias[...]).astype(jnp.bfloat16)
        flat_s[pl.ds(at, step), :] = flat
        proj = lax.dot_general(
            wt, flat, (((1,), (1,)), ((), ())), preferred_element_type=jnp.float32
        )
        ab_s[0, :, pl.ds(at, step)] = (
            jax.nn.sigmoid(proj[hidden : 2 * hidden]) * proj[:hidden]
        )
        ab_s[1, :, pl.ds(at, step)] = (
            jax.nn.sigmoid(proj[3 * hidden :]) * proj[2 * hidden : 3 * hidden]
        )
        return _

    lax.fori_loop(0, 5, project, 0)

    each = 8 // own

    def split(p, _):
        at = pl.multiple_of(p * 8, 8)
        a8, b8 = ab_s[0, pl.ds(at, 8), :], ab_s[1, pl.ds(at, 8), :]
        for e in range(each):
            pick = slice(e * own, (e + 1) * own)
            x_s[p * each + e] = jnp.concatenate([a8[pick], b8[pick]], axis=0).astype(jnp.bfloat16)
        return _

    lax.fori_loop(0, hidden // 8, split, 0)
    pl.semaphore_wait(barrier, n - 1)

    def copy_in(d, src):
        return pltpu.make_async_remote_copy(
            src_ref=x_s.at[d], dst_ref=recv_s.at[src], send_sem=send1.at[d],
            recv_sem=recv1.at[src], device_id=(d // n_rj, lax.rem(d, n_rj)), device_id_type=MESH,
        )

    def copy_back(d, src):
        return pltpu.make_async_remote_copy(
            src_ref=t_s.at[d], dst_ref=out_ref.at[src], send_sem=send2.at[d],
            recv_sem=recv2.at[src], device_id=(d // n_rj, lax.rem(d, n_rj)), device_id_type=MESH,
        )

    def send(d, _):
        copy_in(other(d), me).start()
        return _

    lax.fori_loop(1, n, send, 0)

    def gates(i, _):
        at = pl.multiple_of(i * step, LANES)
        gate_ref[pl.ds(at, step), :] = jax.nn.sigmoid(
            jnp.dot(flat_s[pl.ds(at, step), :], w_gate[...], preferred_element_type=jnp.float32)
        ).astype(jnp.bfloat16)
        return _

    lax.fori_loop(0, 5, gates, 0)

    lane = lax.broadcasted_iota(jnp.int32, (2 * own, LANES), 1)

    def unpack(block, src):
        i0 = (src // n_rj) * rows
        j = lax.rem(src, n_rj)
        wide = block.astype(jnp.float32)
        vregs = [wide[:, v * LANES : (v + 1) * LANES] for v in range(spots // LANES)]
        for k in range(rows):
            start = k * cols
            val = shifted(vregs, start)
            have = LANES - start % LANES
            if have < cols:
                val = jnp.where(
                    lane < have, val, pltpu.roll(vregs[start // LANES + 1], have, 1)
                )
            g_s[j, pl.ds(i0 + k, 2 * own, stride=depth), :] = val

    unpack(x_s[me], me)

    def take(d, _):
        src = lax.rem(me + n - d, n)
        copy_in(src, src).wait_recv()
        unpack(recv_s[src], src)
        return _

    lax.fori_loop(1, n, take, 0)

    for c in range(own):
        for q in range(n_rj):
            b_s[c, :, q * LANES : (q + 1) * LANES] = g_s[
                q, (own + c) * depth : (own + c + 1) * depth, :
            ].astype(jnp.bfloat16)

    lane_o = lax.broadcasted_iota(jnp.int32, (own, LANES), 1)

    def emit(pp, _):
        p = lax.rem(pp + n_rj // 2 + ri // halves, n_rj)
        for c in range(own):
            lhs = g_s[p, c * depth : (c + 1) * depth, :].astype(jnp.bfloat16)
            product = lax.dot_general(
                lhs, b_s[c], (((0,), (0,)), ((), ())), preferred_element_type=jnp.float32
            )
            for q in range(n_rj):
                o_s[q, c * LANES : (c + 1) * LANES, :] = product[:, q * LANES : (q + 1) * LANES]

        def deliver(s, _):
            h, q = s // n_rj, lax.rem(s + rj, n_rj)
            d = (p * halves + h) * n_rj + q
            got = [
                o_s[q, pl.ds(h * rows + r, own, stride=LANES), :] for r in range(rows)
            ]
            pieces = []
            for v in range(spots // LANES):
                piece = None
                for r in range((v * LANES) // cols, min(rows, ((v + 1) * LANES - 1) // cols + 1)):
                    at = r * cols - v * LANES
                    val = pltpu.roll(got[r], at % LANES, 1) if at % LANES else got[r]
                    piece = val if piece is None else jnp.where(lane_o >= at, val, piece)
                pieces.append(piece)
            t_s[d] = jnp.concatenate(pieces, axis=1).astype(jnp.bfloat16)

            @pl.when(d != me)
            def start():
                copy_back(d, me).start()

            return _

        lax.fori_loop(0, halves * n_rj, deliver, 0)
        return _

    lax.fori_loop(0, n_rj, emit, 0)
    mine = pltpu.make_async_copy(t_s.at[me], out_ref.at[me], loc)
    mine.start()

    def finish(d, _):
        src = lax.rem(me + n - d, n)
        to = other(d)
        copy_in(to, me).wait_send()
        copy_back(to, me).wait_send()
        copy_back(src, src).wait_recv()
        return _

    lax.fori_loop(1, n, finish, 0)
    mine.wait()


def exchange(n_ri, n_rj, rows, cols, own, pair, gain, bias, w_in, w_gate):
    n = n_ri * n_rj
    spots, chans = pair.shape
    depth = n_ri * rows
    hidden = n * own
    vmem = pl.BlockSpec(memory_space=pltpu.VMEM)
    return pl.pallas_call(
        functools.partial(body, n_ri, n_rj, rows, cols, own),
        out_shape=(
            jax.ShapeDtypeStruct((spots, chans), jnp.bfloat16),
            jax.ShapeDtypeStruct((n, own, spots), jnp.bfloat16),
        ),
        in_specs=[vmem] * 5,
        out_specs=(vmem, vmem),
        scratch_shapes=[
            pltpu.VMEM((spots, chans), jnp.bfloat16),
            pltpu.VMEM((2, hidden, spots), jnp.float32),
            pltpu.VMEM((n, 2 * own, spots), jnp.bfloat16),
            pltpu.VMEM((n, 2 * own, spots), jnp.bfloat16),
            pltpu.VMEM((n_rj, 2 * own * depth, LANES), jnp.float32),
            pltpu.VMEM((own, depth, n_rj * LANES), jnp.bfloat16),
            pltpu.VMEM((n_rj, own * LANES, LANES), jnp.float32),
            pltpu.VMEM((n, own, spots), jnp.bfloat16),
            pltpu.SemaphoreType.DMA((n,)),
            pltpu.SemaphoreType.DMA((n,)),
            pltpu.SemaphoreType.DMA((n,)),
            pltpu.SemaphoreType.DMA((n,)),
            pltpu.SemaphoreType.DMA,
        ],
        compiler_params=pltpu.CompilerParams(
            collective_id=0, has_side_effects=True, vmem_limit_bytes=56 << 20
        ),
    )(pair, gain, bias, w_in, w_gate)


def local(n_ri, n_rj, pair, in_gain, in_bias, w_in, w_gate, out_gain, out_bias, w_out):
    rows, cols, chans = pair.shape
    hidden = w_out.shape[0]
    n = n_ri * n_rj
    own = hidden // n
    spots = rows * cols
    gate, tri = exchange(
        n_ri, n_rj, rows, cols, own, pair.reshape(spots, chans),
        in_gain[None], in_bias[None], w_in, w_gate,
    )
    tri = tri.reshape(hidden, spots).astype(jnp.float32)
    mean = jnp.mean(tri, axis=0, keepdims=True)
    centered = tri - mean
    var = jnp.mean(centered * centered, axis=0, keepdims=True)
    tri_normed = (
        centered * lax.rsqrt(var + 1e-05) * out_gain[:, None] + out_bias[:, None]
    ).astype(jnp.bfloat16)
    mixed = lax.dot_general(
        tri_normed, w_out, (((0,), (0,)), ((), ())), preferred_element_type=jnp.float32
    )
    update = gate.astype(jnp.float32) * mixed
    return update.reshape(rows, cols, chans).astype(jnp.bfloat16)


def solution(mesh):
    n_ri, n_rj = mesh.shape["ri"], mesh.shape["rj"]
    return jax.shard_map(
        lambda *args: local(n_ri, n_rj, *args),
        mesh=mesh,
        in_specs=(P("ri", "rj", None), P(), P(), P(), P(), P(), P(), P()),
        out_specs=P("ri", "rj", None),
        check_vma=False,
    )
```

```python
import functools

import jax
import jax.numpy as jnp
from jax import lax
from jax.experimental import pallas as pl
from jax.experimental.pallas import tpu as pltpu
from jax.sharding import PartitionSpec as P

MESH = pl.DeviceIdType.MESH
LANES = 128
PARTS = 2


def shifted(vregs, start):
    at, by = divmod(start, LANES)
    if by == 0:
        return vregs[at]
    return pltpu.roll(vregs[at], LANES - by, 1)


def body(n_ri, n_rj, rows, cols, parts, own, pair, gain, bias, w_in, w_gate, gate_ref, out_ref,
         flat_s, ab_s, x_s, recv_s, g_s, b_s, o_s, t_s,
         send1, recv1, send2, recv2, loc):
    n = n_ri * n_rj
    spots = rows * cols
    side = n_ri // 2
    team = n // 2
    depth = side * rows
    wide_part = team * own
    hidden = parts * wide_part
    halves = cols // rows
    ri, rj = lax.axis_index("ri"), lax.axis_index("rj")
    me = ri * n_rj + rj
    seat = lax.rem(ri, side) * n_rj + rj
    base = (ri // side) * side

    def other(d):
        return lax.rem(me + d, n)

    barrier = pltpu.get_barrier_semaphore()

    def greet(d, _):
        to = other(d)
        pl.semaphore_signal(
            barrier, inc=1, device_id=(to // n_rj, lax.rem(to, n_rj)), device_id_type=MESH
        )
        return _

    lax.fori_loop(1, n, greet, 0)

    wt = w_in[...].T
    step = spots // 5

    def project(i, _):
        at = pl.multiple_of(i * step, LANES)
        x = pair[pl.ds(at, step), :].astype(jnp.float32)
        mean = jnp.mean(x, axis=-1, keepdims=True)
        centered = x - mean
        var = jnp.mean(centered * centered, axis=-1, keepdims=True)
        flat = (centered * lax.rsqrt(var + 1e-05) * gain[...] + bias[...]).astype(jnp.bfloat16)
        flat_s[pl.ds(at, step), :] = flat
        proj = lax.dot_general(
            wt, flat, (((1,), (1,)), ((), ())), preferred_element_type=jnp.float32
        )
        ab_s[0, :, pl.ds(at, step)] = (
            jax.nn.sigmoid(proj[hidden : 2 * hidden]) * proj[:hidden]
        )
        ab_s[1, :, pl.ds(at, step)] = (
            jax.nn.sigmoid(proj[3 * hidden :]) * proj[2 * hidden : 3 * hidden]
        )
        return _

    lax.fori_loop(0, 5, project, 0)

    each = 8 // own

    def copy_in(t, d, src):
        return pltpu.make_async_remote_copy(
            src_ref=x_s.at[t, d], dst_ref=recv_s.at[t, src], send_sem=send1.at[t, d],
            recv_sem=recv1.at[t, src], device_id=(base + d // n_rj, lax.rem(d, n_rj)),
            device_id_type=MESH,
        )

    def copy_back(t, d, src):
        return pltpu.make_async_remote_copy(
            src_ref=t_s.at[t, d], dst_ref=out_ref.at[t, src], send_sem=send2.at[t, d],
            recv_sem=recv2.at[t, src], device_id=(d // n_rj, lax.rem(d, n_rj)),
            device_id_type=MESH,
        )

    for t in range(parts):
        def split(p, _):
            at = pl.multiple_of(t * wide_part + p * 8, 8)
            a8, b8 = ab_s[0, pl.ds(at, 8), :], ab_s[1, pl.ds(at, 8), :]
            for e in range(each):
                pick = slice(e * own, (e + 1) * own)
                x_s[t, p * each + e] = jnp.concatenate([a8[pick], b8[pick]], axis=0).astype(
                    jnp.bfloat16
                )
            return _

        lax.fori_loop(0, wide_part // 8, split, 0)
        if t == 0:
            pl.semaphore_wait(barrier, n - 1)

        def send(d, _):
            copy_in(t, lax.rem(seat + d, team), seat).start()
            return _

        lax.fori_loop(1, team, send, 0)

    def gates(i, _):
        at = pl.multiple_of(i * step, LANES)
        gate_ref[pl.ds(at, step), :] = jax.nn.sigmoid(
            jnp.dot(flat_s[pl.ds(at, step), :], w_gate[...], preferred_element_type=jnp.float32)
        ).astype(jnp.bfloat16)
        return _

    lax.fori_loop(0, 5, gates, 0)

    lane = lax.broadcasted_iota(jnp.int32, (2 * own, LANES), 1)

    def unpack(block, src):
        i0 = (src // n_rj) * rows
        j = lax.rem(src, n_rj)
        wide = block.astype(jnp.float32)
        vregs = [wide[:, v * LANES : (v + 1) * LANES] for v in range(spots // LANES)]
        for k in range(rows):
            start = k * cols
            val = shifted(vregs, start)
            have = LANES - start % LANES
            if have < cols:
                val = jnp.where(
                    lane < have, val, pltpu.roll(vregs[start // LANES + 1], have, 1)
                )
            g_s[j, pl.ds(i0 + k, 2 * own, stride=depth), :] = val

    lane_o = lax.broadcasted_iota(jnp.int32, (own, LANES), 1)

    for t in range(parts):
        unpack(x_s[t, seat], seat)

        def take(d, _):
            src = lax.rem(seat + team - d, team)
            copy_in(t, src, src).wait_recv()
            unpack(recv_s[t, src], src)
            return _

        lax.fori_loop(1, team, take, 0)

        for c in range(own):
            for q in range(n_rj):
                b_s[c, :, q * LANES : (q + 1) * LANES] = g_s[
                    q, (own + c) * depth : (own + c + 1) * depth, :
                ].astype(jnp.bfloat16)

        def emit(pp, _):
            p = lax.rem(pp + n_rj // 2 + ri // halves, n_rj)
            for c in range(own):
                lhs = g_s[p, c * depth : (c + 1) * depth, :].astype(jnp.bfloat16)
                product = lax.dot_general(
                    lhs, b_s[c], (((0,), (0,)), ((), ())), preferred_element_type=jnp.float32
                )
                for q in range(n_rj):
                    o_s[q, c * LANES : (c + 1) * LANES, :] = product[:, q * LANES : (q + 1) * LANES]

            def deliver(s, _):
                h, q = s // n_rj, lax.rem(s + rj, n_rj)
                d = (p * halves + h) * n_rj + q
                got = [
                    o_s[q, pl.ds(h * rows + r, own, stride=LANES), :] for r in range(rows)
                ]
                pieces = []
                for v in range(spots // LANES):
                    piece = None
                    for r in range((v * LANES) // cols, min(rows, ((v + 1) * LANES - 1) // cols + 1)):
                        at = r * cols - v * LANES
                        val = pltpu.roll(got[r], at % LANES, 1) if at % LANES else got[r]
                        piece = val if piece is None else jnp.where(lane_o >= at, val, piece)
                    pieces.append(piece)
                t_s[t, d] = jnp.concatenate(pieces, axis=1).astype(jnp.bfloat16)

                @pl.when(d != me)
                def start():
                    copy_back(t, d, me).start()

                return _

            lax.fori_loop(0, halves * n_rj, deliver, 0)
            return _

        lax.fori_loop(0, n_rj, emit, 0)
        pltpu.make_async_copy(t_s.at[t, me], out_ref.at[t, me], loc.at[t]).start()

    for t in range(parts):
        def sent(d, _):
            copy_in(t, lax.rem(seat + d, team), seat).wait_send()
            return _

        def finish(d, _):
            src = lax.rem(me + n - d, n)
            copy_back(t, other(d), me).wait_send()
            copy_back(t, src, src).wait_recv()
            return _

        lax.fori_loop(1, team, sent, 0)
        lax.fori_loop(1, n, finish, 0)
        pltpu.make_async_copy(t_s.at[t, me], out_ref.at[t, me], loc.at[t]).wait()


def exchange(n_ri, n_rj, rows, cols, parts, own, pair, gain, bias, w_in, w_gate):
    n = n_ri * n_rj
    spots, chans = pair.shape
    team = n // 2
    depth = (n_ri // 2) * rows
    hidden = parts * team * own
    vmem = pl.BlockSpec(memory_space=pltpu.VMEM)
    return pl.pallas_call(
        functools.partial(body, n_ri, n_rj, rows, cols, parts, own),
        out_shape=(
            jax.ShapeDtypeStruct((spots, chans), jnp.bfloat16),
            jax.ShapeDtypeStruct((parts, n, own, spots), jnp.bfloat16),
        ),
        in_specs=[vmem] * 5,
        out_specs=(vmem, vmem),
        scratch_shapes=[
            pltpu.VMEM((spots, chans), jnp.bfloat16),
            pltpu.VMEM((2, hidden, spots), jnp.float32),
            pltpu.VMEM((parts, team, 2 * own, spots), jnp.bfloat16),
            pltpu.VMEM((parts, team, 2 * own, spots), jnp.bfloat16),
            pltpu.VMEM((n_rj, 2 * own * depth, LANES), jnp.float32),
            pltpu.VMEM((own, depth, n_rj * LANES), jnp.bfloat16),
            pltpu.VMEM((n_rj, own * LANES, LANES), jnp.float32),
            pltpu.VMEM((parts, n, own, spots), jnp.bfloat16),
            pltpu.SemaphoreType.DMA((parts, team)),
            pltpu.SemaphoreType.DMA((parts, team)),
            pltpu.SemaphoreType.DMA((parts, n)),
            pltpu.SemaphoreType.DMA((parts, n)),
            pltpu.SemaphoreType.DMA((parts,)),
        ],
        compiler_params=pltpu.CompilerParams(
            collective_id=0, has_side_effects=True, vmem_limit_bytes=56 << 20
        ),
    )(pair, gain, bias, w_in, w_gate)


def local(n_ri, n_rj, pair, in_gain, in_bias, w_in, w_gate, out_gain, out_bias, w_out):
    rows, cols, chans = pair.shape
    hidden = w_out.shape[0]
    n = n_ri * n_rj
    team = n // 2
    parts = min(PARTS, hidden // team)
    own = hidden // (team * parts)
    spots = rows * cols
    gate, tri = exchange(
        n_ri, n_rj, rows, cols, parts, own, pair.reshape(spots, chans),
        in_gain[None], in_bias[None], w_in, w_gate,
    )
    tri = tri.reshape(parts, 2, team * own, spots).astype(jnp.float32)
    tri = (tri[:, 0] + tri[:, 1]).reshape(hidden, spots)
    mean = jnp.mean(tri, axis=0, keepdims=True)
    centered = tri - mean
    var = jnp.mean(centered * centered, axis=0, keepdims=True)
    tri_normed = (
        centered * lax.rsqrt(var + 1e-05) * out_gain[:, None] + out_bias[:, None]
    ).astype(jnp.bfloat16)
    mixed = lax.dot_general(
        tri_normed, w_out, (((0,), (0,)), ((), ())), preferred_element_type=jnp.float32
    )
    update = gate.astype(jnp.float32) * mixed
    return update.reshape(rows, cols, chans).astype(jnp.bfloat16)


def solution(mesh):
    n_ri, n_rj = mesh.shape["ri"], mesh.shape["rj"]
    return jax.shard_map(
        lambda *args: local(n_ri, n_rj, *args),
        mesh=mesh,
        in_specs=(P("ri", "rj", None), P(), P(), P(), P(), P(), P(), P()),
        out_specs=P("ri", "rj", None),
        check_vma=False,
    )
```

```python
import functools

import jax
import jax.numpy as jnp
from jax import lax
from jax.experimental import pallas as pl
from jax.experimental.pallas import tpu as pltpu
from jax.sharding import PartitionSpec as P

MESH = pl.DeviceIdType.MESH
LANES = 128
PARTS = 2


def shifted(vregs, start):
    at, by = divmod(start, LANES)
    if by == 0:
        return vregs[at]
    return pltpu.roll(vregs[at], LANES - by, 1)


def body(n_ri, n_rj, rows, cols, parts, own, pair, gain, bias, w_in, w_gate, gate_ref, tri_ref,
         out_ref, flat_s, ab_s, x_s, recv_s, g_s, b_s, o_s, t_s,
         send1, recv1, send2, recv2, loc):
    n = n_ri * n_rj
    spots = rows * cols
    side = n_ri // 2
    team = n // 2
    depth = side * rows
    wide_part = team * own
    hidden = parts * wide_part
    halves = cols // rows
    ri, rj = lax.axis_index("ri"), lax.axis_index("rj")
    me = ri * n_rj + rj
    seat = lax.rem(ri, side) * n_rj + rj
    base = (ri // side) * side

    def other(d):
        return lax.rem(me + d, n)

    barrier = pltpu.get_barrier_semaphore()

    def greet(d, _):
        to = other(d)
        pl.semaphore_signal(
            barrier, inc=1, device_id=(to // n_rj, lax.rem(to, n_rj)), device_id_type=MESH
        )
        return _

    lax.fori_loop(1, n, greet, 0)

    wt = w_in[...].T
    step = spots // 5

    def project(i, _):
        at = pl.multiple_of(i * step, LANES)
        x = pair[pl.ds(at, step), :].astype(jnp.float32)
        mean = jnp.mean(x, axis=-1, keepdims=True)
        centered = x - mean
        var = jnp.mean(centered * centered, axis=-1, keepdims=True)
        flat = (centered * lax.rsqrt(var + 1e-05) * gain[...] + bias[...]).astype(jnp.bfloat16)
        flat_s[pl.ds(at, step), :] = flat
        proj = lax.dot_general(
            wt, flat, (((1,), (1,)), ((), ())), preferred_element_type=jnp.float32
        )
        ab_s[0, :, pl.ds(at, step)] = (
            jax.nn.sigmoid(proj[hidden : 2 * hidden]) * proj[:hidden]
        )
        ab_s[1, :, pl.ds(at, step)] = (
            jax.nn.sigmoid(proj[3 * hidden :]) * proj[2 * hidden : 3 * hidden]
        )
        return _

    lax.fori_loop(0, 5, project, 0)

    each = 8 // own

    def copy_in(t, d, src):
        return pltpu.make_async_remote_copy(
            src_ref=x_s.at[t, d], dst_ref=recv_s.at[t, src], send_sem=send1.at[t, d],
            recv_sem=recv1.at[t, src], device_id=(base + d // n_rj, lax.rem(d, n_rj)),
            device_id_type=MESH,
        )

    def copy_back(t, d, src):
        return pltpu.make_async_remote_copy(
            src_ref=t_s.at[t, d], dst_ref=out_ref.at[t, src], send_sem=send2.at[t, d],
            recv_sem=recv2.at[t, src], device_id=(d // n_rj, lax.rem(d, n_rj)),
            device_id_type=MESH,
        )

    for t in range(parts):
        def split(p, _):
            at = pl.multiple_of(t * wide_part + p * 8, 8)
            a8, b8 = ab_s[0, pl.ds(at, 8), :], ab_s[1, pl.ds(at, 8), :]
            for e in range(each):
                pick = slice(e * own, (e + 1) * own)
                x_s[t, p * each + e] = jnp.concatenate([a8[pick], b8[pick]], axis=0).astype(
                    jnp.bfloat16
                )
            return _

        lax.fori_loop(0, wide_part // 8, split, 0)
        if t == 0:
            pl.semaphore_wait(barrier, n - 1)

        def send(d, _):
            copy_in(t, lax.rem(seat + d, team), seat).start()
            return _

        lax.fori_loop(1, team, send, 0)

    def gates(i, _):
        at = pl.multiple_of(i * step, LANES)
        gate_ref[pl.ds(at, step), :] = jax.nn.sigmoid(
            jnp.dot(flat_s[pl.ds(at, step), :], w_gate[...], preferred_element_type=jnp.float32)
        ).astype(jnp.bfloat16)
        return _

    lax.fori_loop(0, 5, gates, 0)

    lane = lax.broadcasted_iota(jnp.int32, (2 * own, LANES), 1)

    def unpack(block, src):
        i0 = (src // n_rj) * rows
        j = lax.rem(src, n_rj)
        wide = block.astype(jnp.float32)
        vregs = [wide[:, v * LANES : (v + 1) * LANES] for v in range(spots // LANES)]
        for k in range(rows):
            start = k * cols
            val = shifted(vregs, start)
            have = LANES - start % LANES
            if have < cols:
                val = jnp.where(
                    lane < have, val, pltpu.roll(vregs[start // LANES + 1], have, 1)
                )
            g_s[j, pl.ds(i0 + k, 2 * own, stride=depth), :] = val

    lane_o = lax.broadcasted_iota(jnp.int32, (own, LANES), 1)

    for t in range(parts):
        unpack(x_s[t, seat], seat)

        def take(d, _):
            src = lax.rem(seat + team - d, team)
            copy_in(t, src, src).wait_recv()
            unpack(recv_s[t, src], src)
            return _

        lax.fori_loop(1, team, take, 0)

        for c in range(own):
            for q in range(n_rj):
                b_s[c, :, q * LANES : (q + 1) * LANES] = g_s[
                    q, (own + c) * depth : (own + c + 1) * depth, :
                ].astype(jnp.bfloat16)

        def emit(pp, _):
            p = lax.rem(pp + n_rj // 2 + ri // halves, n_rj)
            for c in range(own):
                lhs = g_s[p, c * depth : (c + 1) * depth, :].astype(jnp.bfloat16)
                product = lax.dot_general(
                    lhs, b_s[c], (((0,), (0,)), ((), ())), preferred_element_type=jnp.float32
                )
                for q in range(n_rj):
                    o_s[q, c * LANES : (c + 1) * LANES, :] = product[:, q * LANES : (q + 1) * LANES]

            def deliver(s, _):
                h, q = s // n_rj, lax.rem(s + rj, n_rj)
                d = (p * halves + h) * n_rj + q
                got = [
                    o_s[q, pl.ds(h * rows + r, own, stride=LANES), :] for r in range(rows)
                ]
                pieces = []
                for v in range(spots // LANES):
                    piece = None
                    for r in range((v * LANES) // cols, min(rows, ((v + 1) * LANES - 1) // cols + 1)):
                        at = r * cols - v * LANES
                        val = pltpu.roll(got[r], at % LANES, 1) if at % LANES else got[r]
                        piece = val if piece is None else jnp.where(lane_o >= at, val, piece)
                    pieces.append(piece)
                t_s[t, d] = jnp.concatenate(pieces, axis=1).astype(jnp.bfloat16)

                @pl.when(d != me)
                def start():
                    copy_back(t, d, me).start()

                return _

            lax.fori_loop(0, halves * n_rj, deliver, 0)
            return _

        lax.fori_loop(0, n_rj, emit, 0)
        pltpu.make_async_copy(t_s.at[t, me], out_ref.at[t, me], loc.at[t]).start()

    for t in range(parts):
        def sent(d, _):
            copy_in(t, lax.rem(seat + d, team), seat).wait_send()
            return _

        def finish(d, _):
            src = lax.rem(me + n - d, n)
            copy_back(t, other(d), me).wait_send()
            copy_back(t, src, src).wait_recv()
            return _

        def merge(p, _):
            at = pl.multiple_of(t * wide_part + p * 8, 8)
            sums = [
                out_ref[t, p * each + e].astype(jnp.float32)
                + out_ref[t, team + p * each + e].astype(jnp.float32)
                for e in range(each)
            ]
            tri_ref[pl.ds(at, 8), :] = jnp.concatenate(sums, axis=0)
            return _

        lax.fori_loop(1, team, sent, 0)
        lax.fori_loop(1, n, finish, 0)
        pltpu.make_async_copy(t_s.at[t, me], out_ref.at[t, me], loc.at[t]).wait()
        lax.fori_loop(0, wide_part // 8, merge, 0)


def exchange(n_ri, n_rj, rows, cols, parts, own, pair, gain, bias, w_in, w_gate):
    n = n_ri * n_rj
    spots, chans = pair.shape
    team = n // 2
    depth = (n_ri // 2) * rows
    hidden = parts * team * own
    vmem = pl.BlockSpec(memory_space=pltpu.VMEM)
    return pl.pallas_call(
        functools.partial(body, n_ri, n_rj, rows, cols, parts, own),
        out_shape=(
            jax.ShapeDtypeStruct((spots, chans), jnp.bfloat16),
            jax.ShapeDtypeStruct((hidden, spots), jnp.float32),
        ),
        in_specs=[vmem] * 5,
        out_specs=(vmem, vmem),
        scratch_shapes=[
            pltpu.VMEM((parts, n, own, spots), jnp.bfloat16),
            pltpu.VMEM((spots, chans), jnp.bfloat16),
            pltpu.VMEM((2, hidden, spots), jnp.float32),
            pltpu.VMEM((parts, team, 2 * own, spots), jnp.bfloat16),
            pltpu.VMEM((parts, team, 2 * own, spots), jnp.bfloat16),
            pltpu.VMEM((n_rj, 2 * own * depth, LANES), jnp.float32),
            pltpu.VMEM((own, depth, n_rj * LANES), jnp.bfloat16),
            pltpu.VMEM((n_rj, own * LANES, LANES), jnp.float32),
            pltpu.VMEM((parts, n, own, spots), jnp.bfloat16),
            pltpu.SemaphoreType.DMA((parts, team)),
            pltpu.SemaphoreType.DMA((parts, team)),
            pltpu.SemaphoreType.DMA((parts, n)),
            pltpu.SemaphoreType.DMA((parts, n)),
            pltpu.SemaphoreType.DMA((parts,)),
        ],
        compiler_params=pltpu.CompilerParams(
            collective_id=0, has_side_effects=True, vmem_limit_bytes=56 << 20
        ),
    )(pair, gain, bias, w_in, w_gate)


def local(n_ri, n_rj, pair, in_gain, in_bias, w_in, w_gate, out_gain, out_bias, w_out):
    rows, cols, chans = pair.shape
    hidden = w_out.shape[0]
    n = n_ri * n_rj
    team = n // 2
    parts = min(PARTS, hidden // team)
    own = hidden // (team * parts)
    spots = rows * cols
    gate, tri = exchange(
        n_ri, n_rj, rows, cols, parts, own, pair.reshape(spots, chans),
        in_gain[None], in_bias[None], w_in, w_gate,
    )
    mean = jnp.mean(tri, axis=0, keepdims=True)
    centered = tri - mean
    var = jnp.mean(centered * centered, axis=0, keepdims=True)
    tri_normed = (
        centered * lax.rsqrt(var + 1e-05) * out_gain[:, None] + out_bias[:, None]
    ).astype(jnp.bfloat16)
    mixed = lax.dot_general(
        tri_normed, w_out, (((0,), (0,)), ((), ())), preferred_element_type=jnp.float32
    )
    update = gate.astype(jnp.float32) * mixed
    return update.reshape(rows, cols, chans).astype(jnp.bfloat16)


def solution(mesh):
    n_ri, n_rj = mesh.shape["ri"], mesh.shape["rj"]
    return jax.shard_map(
        lambda *args: local(n_ri, n_rj, *args),
        mesh=mesh,
        in_specs=(P("ri", "rj", None), P(), P(), P(), P(), P(), P(), P()),
        out_specs=P("ri", "rj", None),
        check_vma=False,
    )
```

```python
import functools

import jax
import jax.numpy as jnp
from jax import lax
from jax.experimental import pallas as pl
from jax.experimental.pallas import tpu as pltpu
from jax.sharding import PartitionSpec as P

MESH = pl.DeviceIdType.MESH
LANES = 128
PARTS = 2


def shifted(vregs, start):
    at, by = divmod(start, LANES)
    if by == 0:
        return vregs[at]
    return pltpu.roll(vregs[at], LANES - by, 1)


def body(n_ri, n_rj, rows, cols, parts, own, pair, gain, bias, w_in, w_gate, gate_ref, tri_ref,
         out_ref, flat_s, ab_s, x_s, recv_s, g_s, b_s, o_s, t_s,
         send1, recv1, send2, recv2, loc):
    n = n_ri * n_rj
    spots = rows * cols
    side = n_ri // 2
    team = n // 2
    depth = side * rows
    wide_part = team * own
    hidden = parts * wide_part
    halves = cols // rows
    ri, rj = lax.axis_index("ri"), lax.axis_index("rj")
    me = ri * n_rj + rj
    seat = lax.rem(ri, side) * n_rj + rj
    base = (ri // side) * side

    def other(d):
        return lax.rem(me + d, n)

    barrier = pltpu.get_barrier_semaphore()

    def greet(d, _):
        to = other(d)
        pl.semaphore_signal(
            barrier, inc=1, device_id=(to // n_rj, lax.rem(to, n_rj)), device_id_type=MESH
        )
        return _

    lax.fori_loop(1, n, greet, 0)

    wt = w_in[...].T
    step = spots // 5

    def project(i, _):
        at = pl.multiple_of(i * step, LANES)
        x = pair[pl.ds(at, step), :].astype(jnp.float32)
        mean = jnp.mean(x, axis=-1, keepdims=True)
        centered = x - mean
        var = jnp.mean(centered * centered, axis=-1, keepdims=True)
        flat = (centered * lax.rsqrt(var + 1e-05) * gain[...] + bias[...]).astype(jnp.bfloat16)
        flat_s[pl.ds(at, step), :] = flat
        proj = lax.dot_general(
            wt, flat, (((1,), (1,)), ((), ())), preferred_element_type=jnp.float32
        )
        ab_s[0, :, pl.ds(at, step)] = (
            jax.nn.sigmoid(proj[hidden : 2 * hidden]) * proj[:hidden]
        )
        ab_s[1, :, pl.ds(at, step)] = (
            jax.nn.sigmoid(proj[3 * hidden :]) * proj[2 * hidden : 3 * hidden]
        )
        return _

    lax.fori_loop(0, 5, project, 0)

    each = 8 // own

    def copy_in(t, d, src):
        return pltpu.make_async_remote_copy(
            src_ref=x_s.at[t, d], dst_ref=recv_s.at[t, src], send_sem=send1.at[t, d],
            recv_sem=recv1.at[t, src], device_id=(base + d // n_rj, lax.rem(d, n_rj)),
            device_id_type=MESH,
        )

    def copy_back(t, d, src):
        return pltpu.make_async_remote_copy(
            src_ref=t_s.at[t, d], dst_ref=out_ref.at[t, src], send_sem=send2.at[t, d],
            recv_sem=recv2.at[t, src], device_id=(d // n_rj, lax.rem(d, n_rj)),
            device_id_type=MESH,
        )

    for t in range(parts):
        def split(p, _):
            at = pl.multiple_of(t * wide_part + p * 8, 8)
            a8, b8 = ab_s[0, pl.ds(at, 8), :], ab_s[1, pl.ds(at, 8), :]
            for e in range(each):
                pick = slice(e * own, (e + 1) * own)
                x_s[t, p * each + e] = jnp.concatenate([a8[pick], b8[pick]], axis=0).astype(
                    jnp.bfloat16
                )
            return _

        lax.fori_loop(0, wide_part // 8, split, 0)
        if t == 0:
            pl.semaphore_wait(barrier, n - 1)

        def send(d, _):
            copy_in(t, lax.rem(seat + d, team), seat).start()
            return _

        lax.fori_loop(1, team, send, 0)

    def gates(i, _):
        at = pl.multiple_of(i * step, LANES)
        gate_ref[pl.ds(at, step), :] = jax.nn.sigmoid(
            jnp.dot(flat_s[pl.ds(at, step), :], w_gate[...], preferred_element_type=jnp.float32)
        ).astype(jnp.bfloat16)
        return _

    lax.fori_loop(0, 5, gates, 0)

    lane = lax.broadcasted_iota(jnp.int32, (2 * own, LANES), 1)

    def unpack(block, src):
        i0 = (src // n_rj) * rows
        j = lax.rem(src, n_rj)
        wide = block.astype(jnp.float32)
        vregs = [wide[:, v * LANES : (v + 1) * LANES] for v in range(spots // LANES)]
        for k in range(rows):
            start = k * cols
            val = shifted(vregs, start)
            have = LANES - start % LANES
            if have < cols:
                val = jnp.where(
                    lane < have, val, pltpu.roll(vregs[start // LANES + 1], have, 1)
                )
            g_s[j, pl.ds(i0 + k, 2 * own, stride=depth), :] = val

    lane_o = lax.broadcasted_iota(jnp.int32, (own, LANES), 1)

    for t in range(parts):
        unpack(x_s[t, seat], seat)

        def take(d, _):
            src = lax.rem(seat + team - d, team)
            copy_in(t, src, src).wait_recv()
            unpack(recv_s[t, src], src)
            return _

        lax.fori_loop(1, team, take, 0)

        for c in range(own):
            for q in range(n_rj):
                b_s[c, :, q * LANES : (q + 1) * LANES] = g_s[
                    q, (own + c) * depth : (own + c + 1) * depth, :
                ].astype(jnp.bfloat16)

        def emit(pp, _):
            p = lax.rem(pp + n_rj // 2 + ri // halves, n_rj)
            for c in range(own):
                lhs = g_s[p, c * depth : (c + 1) * depth, :].astype(jnp.bfloat16)
                product = lax.dot_general(
                    lhs, b_s[c], (((0,), (0,)), ((), ())), preferred_element_type=jnp.float32
                )
                for q in range(n_rj):
                    o_s[q, c * LANES : (c + 1) * LANES, :] = product[:, q * LANES : (q + 1) * LANES]

            def deliver(s, _):
                h, q = s // n_rj, lax.rem(s + rj, n_rj)
                d = (p * halves + h) * n_rj + q
                got = [
                    o_s[q, pl.ds(h * rows + r, own, stride=LANES), :] for r in range(rows)
                ]
                pieces = []
                for v in range(spots // LANES):
                    piece = None
                    for r in range((v * LANES) // cols, min(rows, ((v + 1) * LANES - 1) // cols + 1)):
                        at = r * cols - v * LANES
                        val = pltpu.roll(got[r], at % LANES, 1) if at % LANES else got[r]
                        piece = val if piece is None else jnp.where(lane_o >= at, val, piece)
                    pieces.append(piece)
                t_s[t, d] = jnp.concatenate(pieces, axis=1).astype(jnp.bfloat16)

                @pl.when(d != me)
                def start():
                    copy_back(t, d, me).start()

                return _

            lax.fori_loop(0, halves * n_rj, deliver, 0)
            return _

        lax.fori_loop(0, n_rj, emit, 0)
        pltpu.make_async_copy(t_s.at[t, me], out_ref.at[t, me], loc.at[t]).start()

    for t in range(parts):
        def sent(d, _):
            copy_in(t, lax.rem(seat + d, team), seat).wait_send()
            return _

        def finish(d, _):
            src = lax.rem(me + n - d, n)
            copy_back(t, other(d), me).wait_send()
            copy_back(t, src, src).wait_recv()
            return _

        def merge(p, _):
            at = pl.multiple_of(t * wide_part + p * 8, 8)
            sums = [
                out_ref[t, p * each + e].astype(jnp.float32)
                + out_ref[t, team + p * each + e].astype(jnp.float32)
                for e in range(each)
            ]
            tri_ref[pl.ds(at, 8), :] = jnp.concatenate(sums, axis=0)
            return _

        lax.fori_loop(1, team, sent, 0)
        lax.fori_loop(1, n, finish, 0)
        pltpu.make_async_copy(t_s.at[t, me], out_ref.at[t, me], loc.at[t]).wait()
        lax.fori_loop(0, wide_part // 8, merge, 0)

    def normalize(i, _):
        at = pl.multiple_of(i * step, LANES)
        x = tri_ref[:, pl.ds(at, step)]
        mean = jnp.mean(x, axis=0, keepdims=True)
        centered = x - mean
        var = jnp.mean(centered * centered, axis=0, keepdims=True)
        tri_ref[:, pl.ds(at, step)] = centered * lax.rsqrt(var + 1e-05)
        return _

    lax.fori_loop(0, 5, normalize, 0)


def exchange(n_ri, n_rj, rows, cols, parts, own, pair, gain, bias, w_in, w_gate):
    n = n_ri * n_rj
    spots, chans = pair.shape
    team = n // 2
    depth = (n_ri // 2) * rows
    hidden = parts * team * own
    vmem = pl.BlockSpec(memory_space=pltpu.VMEM)
    return pl.pallas_call(
        functools.partial(body, n_ri, n_rj, rows, cols, parts, own),
        out_shape=(
            jax.ShapeDtypeStruct((spots, chans), jnp.bfloat16),
            jax.ShapeDtypeStruct((hidden, spots), jnp.float32),
        ),
        in_specs=[vmem] * 5,
        out_specs=(vmem, vmem),
        scratch_shapes=[
            pltpu.VMEM((parts, n, own, spots), jnp.bfloat16),
            pltpu.VMEM((spots, chans), jnp.bfloat16),
            pltpu.VMEM((2, hidden, spots), jnp.float32),
            pltpu.VMEM((parts, team, 2 * own, spots), jnp.bfloat16),
            pltpu.VMEM((parts, team, 2 * own, spots), jnp.bfloat16),
            pltpu.VMEM((n_rj, 2 * own * depth, LANES), jnp.float32),
            pltpu.VMEM((own, depth, n_rj * LANES), jnp.bfloat16),
            pltpu.VMEM((n_rj, own * LANES, LANES), jnp.float32),
            pltpu.VMEM((parts, n, own, spots), jnp.bfloat16),
            pltpu.SemaphoreType.DMA((parts, team)),
            pltpu.SemaphoreType.DMA((parts, team)),
            pltpu.SemaphoreType.DMA((parts, n)),
            pltpu.SemaphoreType.DMA((parts, n)),
            pltpu.SemaphoreType.DMA((parts,)),
        ],
        compiler_params=pltpu.CompilerParams(
            collective_id=0, has_side_effects=True, vmem_limit_bytes=56 << 20
        ),
    )(pair, gain, bias, w_in, w_gate)


def local(n_ri, n_rj, pair, in_gain, in_bias, w_in, w_gate, out_gain, out_bias, w_out):
    rows, cols, chans = pair.shape
    hidden = w_out.shape[0]
    n = n_ri * n_rj
    team = n // 2
    parts = min(PARTS, hidden // team)
    own = hidden // (team * parts)
    spots = rows * cols
    gate, tri = exchange(
        n_ri, n_rj, rows, cols, parts, own, pair.reshape(spots, chans),
        in_gain[None], in_bias[None], w_in, w_gate,
    )
    tri_normed = (tri * out_gain[:, None] + out_bias[:, None]).astype(jnp.bfloat16)
    mixed = lax.dot_general(
        tri_normed, w_out, (((0,), (0,)), ((), ())), preferred_element_type=jnp.float32
    )
    update = gate.astype(jnp.float32) * mixed
    return update.reshape(rows, cols, chans).astype(jnp.bfloat16)


def solution(mesh):
    n_ri, n_rj = mesh.shape["ri"], mesh.shape["rj"]
    return jax.shard_map(
        lambda *args: local(n_ri, n_rj, *args),
        mesh=mesh,
        in_specs=(P("ri", "rj", None), P(), P(), P(), P(), P(), P(), P()),
        out_specs=P("ri", "rj", None),
        check_vma=False,
    )
```
